256 devices in a mesh: req: 32 (over z, x), mlp: 8 (over y, core).
Axes of the slice: x: 4, y: 4, z: 8, core: 2. Of those that a mesh axis runs over, the one named last changes fastest.
Arguments:
- tokens: bfloat16 [8192, 2048], P('req', 'mlp'), may hold values from -12 to 12
- segment_ids: int32 [8192], P('req'), may hold values from 0 to 16, never falling along the last dimension, each value on 1 to 4096 neighbouring positions
- page_source: int32 [512], P('req'), may hold values from 0 to 511, each once
- query_weight: bfloat16 [2048, 2048], P(None, 'mlp')
- key_weight: bfloat16 [2048, 2048], P(None, 'mlp')
- value_weight: bfloat16 [2048, 2048], P(None, 'mlp'), may hold values from -0.125 to 0.125
- out_weight: bfloat16 [2048, 2048], P('mlp')
- query_gain: float32 [2048], P('mlp'), may hold values from 0.5 to 9
- key_gain: float32 [2048], P('mlp'), may hold values from 0.5 to 9
- attention_gain: float32 [2048], P('mlp'), may hold values from 0.25 to 1.75
- gate_weight: bfloat16 [2048, 8192], P('req', 'mlp'), may hold values from -0.125 to 0.125
- up_weight: bfloat16 [2048, 8192], P('req', 'mlp'), may hold values from -0.125 to 0.125
- down_weight: bfloat16 [2048, 8192], P('req', 'mlp')
- feedforward_gain: float32 [2048], P('mlp'), may hold values from 0.25 to 1.75
Outputs:
- layer_out: bfloat16 [8192, 2048], P('req', 'mlp')
- page_cache: bfloat16 [512, 2, 16, 2048], P('req', None, None, 'mlp')
The draws below stay inside these ranges and needn't reach their ends.
Inputs may be any that keep to these rules, and one draw needn't show every extreme that they name: `segment_ids`: segment ids never fall along the stream; each prompt has 1 to 4096 tokens and one has exactly 4096. `page_source`: each stream page appears once.
All inputs are finite; a program needn't handle non-finite values.
Results may differ from the reference program's by a relative error of at most 0.019.
The reference program's roundings to bfloat16 on the way (of `attended`, `residual` and `hidden`) count: a program that leaves them out, or rounds other values in their place, can miss the bound.
Values may be sent and summed in bfloat16 or wider, within the bound.
No kernel may reach another device: no remote copies, remote signals or barrier semaphores. Data moves between devices by JAX's collectives and lax.ppermute only.
A program may use at most 128 MiB of HBM per device.

```python
import math
import jax
import jax.numpy as jnp
import numpy as np
from jax import lax

D = 2048
H = 16
HD = 128
FF = 8192
PAGE = 16
TOK_DEV = 256
TOKENS = 8192
SEGS = 17
LONG = 4096
PAGES = 512


def trend_scale(rng_key, size_n):
    position_frac = jnp.arange(size_n, dtype=jnp.float32) / size_n
    random_part = jnp.exp(jax.random.uniform(rng_key, (size_n,), jnp.float32, 0.0, math.log(4.0)))
    return jnp.exp(position_frac * math.log(3.0)) * random_part


def projection(rng_key, fan_in, shape, out_dim):
    first_key, second_key = jax.random.split(rng_key)
    base_vals = jnp.clip(jax.random.normal(first_key, shape, jnp.float32), -4.0, 4.0)
    scales = trend_scale(second_key, shape[out_dim])
    if out_dim == 1:
        scaled = base_vals * scales[None, :]
    else:
        scaled = base_vals * scales[:, None]
    return (scaled / math.sqrt(fan_in)).astype(jnp.bfloat16)


def head_gain(rng_key, salt):
    feature_key = jax.random.fold_in(rng_key, salt)
    noise = jnp.clip(jax.random.normal(feature_key, (D,), jnp.float32), -3.0, 3.0)
    return 1.0 + 0.15 * noise


def draw_tokens(key, part):
    first_key, second_key = jax.random.split(jax.random.fold_in(key, 11))
    base_vals = jnp.clip(jax.random.normal(first_key, (TOKENS, D), jnp.float32), -4.0, 4.0)
    row_scale = jnp.exp(jax.random.uniform(second_key, (TOKENS, 1), jnp.float32, math.log(0.3), math.log(3.0)))
    return (base_vals * row_scale).astype(jnp.bfloat16)


def draw_query_weight(key, part):
    return projection(jax.random.fold_in(key, 21), D, (D, D), 1)


def draw_key_weight(key, part):
    return projection(jax.random.fold_in(key, 22), D, (D, D), 1)


def draw_out_weight(key, part):
    return projection(jax.random.fold_in(key, 23), D, (D, D), 1)


def draw_down_weight(key, part):
    return projection(jax.random.fold_in(key, 24), FF, (D, FF), 0)


def draw_query_gain(key, part):
    return head_gain(key, 31)


def draw_key_gain(key, part):
    return head_gain(key, 32)


def block_levels(stream_key, shape, pieces, smallest, high):
    level, own = 1.0, jax.random.fold_in(stream_key, 6)
    for dim, blocks in pieces:
        draws = jnp.exp(jax.random.uniform(jax.random.fold_in(own, dim), (blocks,), jnp.float32, smallest / len(pieces), high / len(pieces)))
        level = level * jnp.repeat(draws, shape[dim] // blocks).reshape([-1 if axis == dim else 1 for axis in range(len(shape))])
    return level


def split_up(amount, total, bound, skew):
    portions = [(1 << 20) // math.isqrt(grade ** skew) + 1 for grade in range(2, amount + 1)]
    rest, holding = total - bound - (amount - 1), [1] * (amount - 1)
    while rest > 0:
        candidates = [i for i in range(amount - 1) if holding[i] < bound]
        whole, left = sum([portions[i] for i in candidates]), rest
        for i in candidates:
            extra = min(bound - holding[i], max(1, left * portions[i] // whole), rest)
            holding[i] = holding[i] + extra
            rest = rest - extra
    return np.array([bound] + holding)


def ragged(rng, number_of, total, most, slope):
    if number_of == 2:
        one = jax.random.randint(rng, (), max(1, total - most), min(most, total - 1) + 1)
        return jnp.stack([one, total - one])
    lengths = jnp.asarray(split_up(number_of, total, most, slope), jnp.int32)
    twos = (number_of - 1) // 2
    giver, sink = lengths[1:1 + 2 * twos:2], lengths[2:2 + 2 * twos:2]
    slack = jnp.minimum(giver - 1, most - sink)
    passed = jax.random.randint(jax.random.fold_in(rng, 1), (twos,), 0, 1 << 20) % (slack + 1)
    lengths = lengths.at[1:1 + 2 * twos:2].set(giver - passed).at[2:2 + 2 * twos:2].set(sink + passed)
    return lengths[jax.random.permutation(jax.random.fold_in(rng, 2), number_of)]


def normal_values(stream_key, dims, scale, bound, shards=(), kind=jnp.bfloat16):
    gain = block_levels(stream_key, dims, shards, -0.22, 0.18) if shards else 1.0
    drawn = jax.random.normal(stream_key, dims, jnp.float32) * scale * gain
    return jnp.minimum(jnp.maximum(drawn, -bound), bound).astype(kind)


def setup_inputs(seed: int = 0) -> dict:
    streams_of = jax.random.split(jax.random.key(seed), 15)
    return {
        "tokens": draw_tokens(jax.random.fold_in(streams_of[14], 71), 0),
        "segment_ids": jnp.searchsorted(jnp.cumsum(ragged(streams_of[1], SEGS, TOKENS, LONG, 1)), jnp.arange(TOKENS), side="right").astype(jnp.int32),
        "page_source": jax.random.permutation(streams_of[2], PAGES).astype(jnp.int32),
        "query_weight": draw_query_weight(jax.random.fold_in(streams_of[14], 71), 0),
        "key_weight": draw_key_weight(jax.random.fold_in(streams_of[14], 71), 0),
        "value_weight": normal_values(streams_of[5], (D, D), D ** -0.5, 0.125, ((1, 8),)),
        "out_weight": draw_out_weight(jax.random.fold_in(streams_of[14], 71), 0),
        "query_gain": draw_query_gain(jax.random.fold_in(streams_of[14], 71), 0),
        "key_gain": draw_key_gain(jax.random.fold_in(streams_of[14], 71), 0),
        "attention_gain": jnp.clip(1.0 + 0.15 * jax.random.normal(streams_of[9], (D,), jnp.float32), 0.25, 1.75),
        "gate_weight": normal_values(streams_of[10], (D, FF), D ** -0.5, 0.125, ((0, 32), (1, 8))),
        "up_weight": normal_values(streams_of[11], (D, FF), D ** -0.5, 0.125, ((0, 32), (1, 8))),
        "down_weight": draw_down_weight(jax.random.fold_in(streams_of[14], 71), 0),
        "feedforward_gain": jnp.clip(1.0 + 0.15 * jax.random.normal(streams_of[13], (D,), jnp.float32), 0.25, 1.75),
    }


rope_base = 500000.0
norm_eps = 1e-06

def rope_tables(positions, head_dim):
    half_dim = head_dim // 2
    inv_freq = rope_base ** (-(jnp.arange(half_dim, dtype=jnp.float32) * 2.0) / head_dim)
    angles = positions.astype(jnp.float32)[:, None] * inv_freq[None, :]
    return (jnp.cos(angles), jnp.sin(angles))

def rotate(values, cosine_table, sine_table, head_dim):
    tok_rows = values.shape[0]
    head_count = values.shape[1] // head_dim
    shaped = values.reshape(tok_rows, head_count, head_dim)
    half_dim = head_dim // 2
    first_half = shaped[..., :half_dim]
    second = shaped[..., half_dim:]
    cos_b = cosine_table[:, None, :]
    sin_b = sine_table[:, None, :]
    turned = jnp.concatenate([first_half * cos_b - second * sin_b, second * cos_b + first_half * sin_b], axis=-1)
    return turned.reshape(tok_rows, head_count * head_dim)

def rms_scale(values, gain_vec):
    mean_square = lax.optimization_barrier(jnp.mean(values * values, axis=1))
    return values * lax.rsqrt(mean_square + norm_eps)[:, None] * gain_vec[None, :]

def reference(tokens, segment_ids, page_source, query_weight, key_weight, value_weight, out_weight, query_gain, key_gain, attention_gain, gate_weight, up_weight, down_weight, feedforward_gain):
    query_proj = jnp.dot(tokens, query_weight, preferred_element_type=jnp.float32)
    key_proj = jnp.dot(tokens, key_weight, preferred_element_type=jnp.float32)
    value_proj = jnp.dot(tokens, value_weight, preferred_element_type=jnp.float32)
    query_n = rms_scale(query_proj, query_gain)
    key_n = rms_scale(key_proj, key_gain)
    seg_range = jnp.arange(SEGS, dtype=jnp.int32)
    matches = segment_ids[:, None] == seg_range[None, :]
    counts = lax.optimization_barrier(jnp.sum(matches.astype(jnp.int32), axis=0)).astype(jnp.int32)
    seg_starts = (jnp.cumsum(counts) - counts).astype(jnp.int32)
    token_index = jnp.arange(TOKENS, dtype=jnp.int32)
    positions = (token_index - seg_starts[segment_ids]).astype(jnp.int32)
    cosine_table, sine_table = rope_tables(positions, HD)
    query_r = rotate(query_n, cosine_table, sine_table, HD).astype(jnp.bfloat16)
    key_r = rotate(key_n, cosine_table, sine_table, HD).astype(jnp.bfloat16)
    value_b = value_proj.astype(jnp.bfloat16)
    score_scale = HD ** (-0.5)
    query_heads = query_r.reshape(TOKENS, H, HD).transpose(1, 0, 2)
    key_heads = key_r.reshape(TOKENS, H, HD).transpose(1, 0, 2)
    value_heads = value_b.reshape(TOKENS, H, HD).transpose(1, 0, 2)
    block_count = TOKENS // TOK_DEV

    def one_head(operands):
        query_h, key_h, value_h = operands

        def one_block(block_index):
            offset = (block_index * TOK_DEV).astype(jnp.int32)
            query_b = lax.dynamic_slice_in_dim(query_h, offset, TOK_DEV, 0)
            seg_b = lax.dynamic_slice_in_dim(segment_ids, offset, TOK_DEV, 0)
            index_b = lax.dynamic_slice_in_dim(token_index, offset, TOK_DEV, 0)
            scores = jnp.dot(query_b, key_h.T, preferred_element_type=jnp.float32) * score_scale
            visible = (seg_b[:, None] == segment_ids[None, :]) & (index_b[:, None] >= token_index[None, :])
            top_score = lax.optimization_barrier(jnp.max(jnp.where(visible, scores, -1e+30), axis=1))
            weights = jnp.where(visible, jnp.exp(scores - top_score[:, None]), 0.0)
            denom = lax.optimization_barrier(jnp.sum(weights, axis=1))
            mixed = jnp.dot(weights.astype(jnp.bfloat16), value_h, preferred_element_type=jnp.float32)
            return (mixed / denom[:, None]).astype(jnp.bfloat16)
        blocks = lax.map(one_block, jnp.arange(block_count, dtype=jnp.int32))
        return blocks.reshape(TOKENS, HD)
    attended_heads = lax.map(one_head, (query_heads, key_heads, value_heads))
    attended = attended_heads.transpose(1, 0, 2).reshape(TOKENS, D)
    projected = jnp.dot(attended, out_weight, preferred_element_type=jnp.float32)
    residual = (tokens.astype(jnp.float32) + rms_scale(projected, attention_gain)).astype(jnp.bfloat16)
    gate_act = jnp.dot(residual, gate_weight, preferred_element_type=jnp.float32)
    up_act = jnp.dot(residual, up_weight, preferred_element_type=jnp.float32)
    hidden = (jax.nn.silu(gate_act) * up_act).astype(jnp.bfloat16)
    down_act = lax.dot_general(hidden, down_weight, (((1,), (1,)), ((), ())), preferred_element_type=jnp.float32)
    layer_out = (residual.astype(jnp.float32) + rms_scale(down_act, feedforward_gain)).astype(jnp.bfloat16)
    key_pages = key_r.reshape(PAGES, PAGE, D)[page_source]
    value_pages = value_b.reshape(PAGES, PAGE, D)[page_source]
    page_cache = jnp.stack([key_pages, value_pages], axis=1)
    return (layer_out, page_cache)
```

```python
import jax
import jax.numpy as jnp
from jax import lax
from jax.sharding import PartitionSpec as P

HD = 128
PAGE = 16


rope_base = 500000.0
norm_eps = 1e-06


def rope_tables(positions, head_dim):
    half_dim = head_dim // 2
    inv_freq = rope_base ** (-(jnp.arange(half_dim, dtype=jnp.float32) * 2.0) / head_dim)
    angles = positions.astype(jnp.float32)[:, None] * inv_freq[None, :]
    return (jnp.cos(angles), jnp.sin(angles))


def rotate(values, cosine_table, sine_table, head_dim):
    tok_rows = values.shape[0]
    head_count = values.shape[1] // head_dim
    shaped = values.reshape(tok_rows, head_count, head_dim)
    half_dim = head_dim // 2
    first_half = shaped[..., :half_dim]
    second = shaped[..., half_dim:]
    cos_b = cosine_table[:, None, :]
    sin_b = sine_table[:, None, :]
    turned = jnp.concatenate(
        [first_half * cos_b - second * sin_b, second * cos_b + first_half * sin_b], axis=-1
    )
    return turned.reshape(tok_rows, head_count * head_dim)


SIDE_X = 4


def req_shift(value, dz, dx):
    size = lax.axis_size("req")
    side_z = size // SIDE_X
    pairs = []
    for source in range(size):
        z, x = source // SIDE_X, source % SIDE_X
        pairs.append((source, (z + dz) % side_z * SIDE_X + (x + dx) % SIDE_X))
    return lax.ppermute(value, "req", pairs)


def spread_z(value):
    side_z = lax.axis_size("req") // SIDE_X
    order = sorted(range(1, side_z), key=lambda k: -min(k, side_z - k))
    return [(0, value)] + [(k, req_shift(value, k, 0)) for k in order]


def spread_x(value):
    return [(0, value)] + [(k, req_shift(value, 0, k)) for k in (2, 1, 3)]


def place(pieces, own, count, dim):
    shape = list(pieces[0][1].shape)
    shape.insert(dim, count)
    whole = jnp.zeros(shape, pieces[0][1].dtype)
    for k, piece in pieces:
        whole = lax.dynamic_update_index_in_dim(whole, piece, (own - k) % count, dim)
    return whole


def gather_z_first(value):
    side_z = lax.axis_size("req") // SIDE_X
    own = lax.axis_index("req")
    block = place(spread_z(value), own // SIDE_X, side_z, 0)
    return place(spread_x(block), own % SIDE_X, SIDE_X, 1)


def gather_x_first(value):
    side_z = lax.axis_size("req") // SIDE_X
    own = lax.axis_index("req")
    block = place(spread_x(value), own % SIDE_X, SIDE_X, 0)
    return place(spread_z(block), own // SIDE_X, side_z, 0)


def req_total(value):
    for dz in (4, 2, 1):
        value = value + req_shift(value, dz, 0)
    for dx in (2, 1):
        value = value + req_shift(value, 0, dx)
    return value


def mlp_shift(value, k):
    size = lax.axis_size("mlp")
    return lax.ppermute(value, "mlp", [(i, (i + k) % size) for i in range(size)])


def mlp_total(value):
    received = [mlp_shift(value, k) for k in range(1, lax.axis_size("mlp"))]
    for other in received:
        value = value + other
    return value


def mlp_scatter(branch_term):
    size = lax.axis_size("mlp")
    own = lax.axis_index("mlp")
    width = branch_term.shape[1] // size
    rounded = branch_term.astype(jnp.bfloat16)

    def block(k):
        return lax.dynamic_slice_in_dim(rounded, (own + k) % size * width, width, 1)

    received = [mlp_shift(block(k), k) for k in range(1, size)]
    total = block(0).astype(jnp.float32)
    for other in received:
        total = total + other.astype(jnp.float32)
    return total


def post_norm(branch_term, gain_vec, model_width):
    own_part = mlp_scatter(branch_term)
    mean_square = mlp_total(jnp.sum(own_part * own_part, axis=1)) / model_width
    return own_part * lax.rsqrt(mean_square + norm_eps)[:, None] * gain_vec[None, :]


def per_device(
    tokens,
    segment_ids,
    page_source,
    query_weight,
    key_weight,
    value_weight,
    out_weight,
    query_gain,
    key_gain,
    attention_gain,
    gate_weight,
    up_weight,
    down_weight,
    feedforward_gain,
):
    tok_rows = tokens.shape[0]
    local_width = tokens.shape[1]
    model_width = query_weight.shape[0]
    head_dim = HD
    head_count = local_width // head_dim
    gate_up = gather_z_first(jnp.stack([gate_weight, up_weight]))
    gate_full = gate_up[:, :, 0].reshape(model_width, -1)
    up_full = gate_up[:, :, 1].reshape(model_width, -1)
    down_full = gather_x_first(down_weight).reshape(model_width, -1)
    full_rows = lax.all_gather(tokens, "mlp", axis=1, tiled=True)
    query_proj = jnp.dot(full_rows, query_weight, preferred_element_type=jnp.float32)
    key_proj = jnp.dot(full_rows, key_weight, preferred_element_type=jnp.float32)
    value_proj = jnp.dot(full_rows, value_weight, preferred_element_type=jnp.float32)
    query_total, key_total = mlp_total(
        jnp.stack([jnp.sum(query_proj * query_proj, axis=1), jnp.sum(key_proj * key_proj, axis=1)])
    )
    query_n = (
        query_proj * lax.rsqrt(query_total / model_width + norm_eps)[:, None] * query_gain[None, :]
    )
    key_n = key_proj * lax.rsqrt(key_total / model_width + norm_eps)[:, None] * key_gain[None, :]
    seg_total = lax.axis_size("req") // 2 + 1
    seg_range = jnp.arange(seg_total, dtype=jnp.int32)
    matches = segment_ids[:, None] == seg_range[None, :]
    counts = jnp.sum(matches.astype(jnp.int32), axis=0)
    totals = req_total(counts)
    seg_starts = jnp.cumsum(totals) - totals
    row_base = lax.axis_index("req") * tok_rows
    global_index = row_base + jnp.arange(tok_rows, dtype=jnp.int32)
    own_start = jnp.sum(jnp.where(matches, seg_starts[None, :], 0), axis=1)
    positions = global_index - own_start
    cosine_table, sine_table = rope_tables(positions, head_dim)
    query_r = rotate(query_n, cosine_table, sine_table, head_dim).astype(jnp.bfloat16)
    key_r = rotate(key_n, cosine_table, sine_table, head_dim).astype(jnp.bfloat16)
    value_b = value_proj.astype(jnp.bfloat16)
    query_heads = query_r.reshape(tok_rows, head_count, head_dim)
    score_scale = head_dim ** (-0.5)
    pages_here = page_source.shape[0]
    page_offsets = jnp.arange(PAGE, dtype=jnp.int32)
    attn_init = (
        jnp.full((head_count, tok_rows), -1e30, jnp.float32),
        jnp.zeros((head_count, tok_rows), jnp.float32),
        jnp.zeros((tok_rows, head_count, head_dim), jnp.float32),
    )
    cache_init = jnp.zeros((pages_here, 2, PAGE, local_width), jnp.bfloat16)
    fold_state = attn_init + (cache_init,)
    fetched = (
        lax.all_gather(key_r, "req", axis=0, tiled=True),
        gather_z_first(value_b).reshape(-1, local_width),
    )
    key_part, value_part = fetched
    row_count = key_part.shape[0]
    block_rows = 512

    def one_block(block_index, state):
        run_max, run_sum, run_out = state
        offset = block_index * block_rows
        key_block = lax.dynamic_slice_in_dim(key_part, offset, block_rows, 0).reshape(
            block_rows, head_count, head_dim
        )
        value_block = lax.dynamic_slice_in_dim(value_part, offset, block_rows, 0).reshape(
            block_rows, head_count, head_dim
        )
        key_index = offset + jnp.arange(block_rows, dtype=jnp.int32)
        visible = (
            (own_start[:, None] <= key_index[None, :])
            & (global_index[:, None] >= key_index[None, :])
        )
        scores = (
            jnp.einsum("thd,rhd->htr", query_heads, key_block, preferred_element_type=jnp.float32)
            * score_scale
        )
        masked = jnp.where(visible[None], scores, -1e30)
        new_max = jnp.maximum(run_max, jnp.max(masked, axis=2))
        weights = jnp.where(visible[None], jnp.exp(scores - new_max[:, :, None]), 0.0)
        factor = jnp.exp(run_max - new_max)
        run_sum = run_sum * factor + jnp.sum(weights, axis=2)
        update = jnp.einsum(
            "htr,rhd->thd",
            weights.astype(jnp.bfloat16),
            value_block,
            preferred_element_type=jnp.float32,
        )
        run_out = run_out * factor.T[:, :, None] + update
        return (new_max, run_sum, run_out)

    attn_state = lax.fori_loop(
        own_start[0] // block_rows,
        (row_base + tok_rows - 1) // block_rows + 1,
        one_block,
        fold_state[:3],
    )
    place_key_part = fetched[0]
    row_count = place_key_part.shape[0]
    page_rows = page_source[:, None] * PAGE + page_offsets[None, :]
    in_piece = (page_rows >= 0) & (page_rows < row_count)
    clipped = jnp.clip(page_rows, 0, row_count - 1)
    stacked = jnp.stack([place_key_part[clipped], fetched[1][clipped]], axis=1)
    page_cache = jnp.where(in_piece[:, None, :, None], stacked, fold_state[3])
    run_max, run_sum, run_out, page_cache = (
        attn_state[0],
        attn_state[1],
        attn_state[2],
        page_cache,
    )
    attended = (run_out / run_sum.T[:, :, None]).reshape(tok_rows, local_width).astype(jnp.bfloat16)
    projected = jnp.dot(attended, out_weight, preferred_element_type=jnp.float32)
    residual = (
        tokens.astype(jnp.float32) + post_norm(projected, attention_gain, model_width)
    ).astype(jnp.bfloat16)
    normed = lax.all_gather(residual, "mlp", axis=1, tiled=True)
    contract = (((1,), (1,)), ((), ()))
    fetched = (gate_full, up_full)
    gate_act = jnp.dot(normed, fetched[0], preferred_element_type=jnp.float32)
    up_act = jnp.dot(normed, fetched[1], preferred_element_type=jnp.float32)
    hidden = (jax.nn.silu(gate_act) * up_act).astype(jnp.bfloat16)
    down_act = lax.dot_general(
        hidden,
        down_full,
        contract,
        preferred_element_type=jnp.float32,
    )
    layer_out = (
        residual.astype(jnp.float32) + post_norm(down_act, feedforward_gain, model_width)
    ).astype(jnp.bfloat16)
    return (layer_out, page_cache)


def solution(mesh):
    in_specs = (
        P("req", "mlp"),
        P("req"),
        P("req"),
        P(None, "mlp"),
        P(None, "mlp"),
        P(None, "mlp"),
        P("mlp", None),
        P("mlp"),
        P("mlp"),
        P("mlp"),
        P("req", "mlp"),
        P("req", "mlp"),
        P("req", "mlp"),
        P("mlp"),
    )
    out_specs = (P("req", "mlp"), P("req", None, None, "mlp"))
    return jax.shard_map(
        per_device, mesh=mesh, in_specs=in_specs, out_specs=out_specs, check_vma=False
    )
```
